32 devices in a mesh: mem: 4 (over y, x), lat: 2 (over core), lon: 4 (over z).
Axes of the slice: x: 2, y: 2, z: 4, core: 2. Of those that a mesh axis runs over, the one named last changes fastest.
Arguments:
- control: bfloat16 [4, 48, 48, 2048], P('mem', None, 'lat', 'lon'), may hold values from -6 to 6
- ens_pert: bfloat16 [4, 48, 48, 2048], P('mem', None, 'lat', 'lon'), may hold values from -6 to 6
- vertical_mix: bfloat16 [48, 48], replicated, may hold values from -0.875 to 0.875
- obs_values: bfloat16 [8, 8, 48, 1024], P(('lat', 'lon')), may hold values from -6 to 6
- obs_cells: int32 [8, 8, 1024], P(('lat', 'lon')), may hold values from 0 to 12287
- obs_counts: int32 [8, 8], P(('lat', 'lon')), may hold values from 256 to 1024, as said below
Outputs:
- increment: float32 [48, 48, 2048], P('mem', 'lat', 'lon')
- gradient: float32 [4, 48, 48, 2048], P('mem', None, 'lat', 'lon')
The draws below stay inside these ranges and needn't reach their ends.
Inputs may be any that keep to these rules, and one draw needn't show every extreme that they name: `obs_counts`: live slots per pair of tiles; for some destination tile every source fills all 1024 slots.
All inputs are finite; a program needn't handle non-finite values.
Results may differ from the reference program's by a relative error of at most 0.0056.
Values may be sent and summed in bfloat16 or wider, within the bound.
A program may use at most 128 MiB of HBM per device.

```python
import math
import jax
import jax.numpy as jnp
from jax import lax

LEV = 48
LATD = 24
LOND = 512
HALF = 24
CAP = 1024
TILES = 8
CELLS = 12288
MEMBERS = 4
NLAT = 48
NLON = 2048
N_LAT = 2
N_LON = 4


def draw_obs_counts(key, part):
    key_heavy = jax.random.fold_in(key, 11)
    key_base = jax.random.fold_in(key, 23)
    key_full = jax.random.fold_in(key, 37)
    heavy_level = jax.random.randint(key_heavy, (TILES,), 0, 4)
    base_count = jax.random.randint(key_base, (TILES, TILES), CAP // 4, CAP + 1)
    scaled = jnp.minimum(base_count + heavy_level[None, :] * (CAP // 4), CAP)
    full_tile = jax.random.randint(key_full, (), 0, TILES)
    return jnp.where(jnp.arange(TILES)[None, :] == full_tile, CAP, scaled).astype(jnp.int32)


def set_ends(drawn, own_key, smallest, largest):
    index_at = [jax.random.randint(jax.random.fold_in(own_key, axis), (), 0, length) for axis, length in enumerate(drawn.shape)]
    widest = drawn.shape.index(max(drawn.shape))
    neighbour = index_at[:widest] + [(index_at[widest] + 1) % drawn.shape[widest]] + index_at[widest + 1:]
    return drawn.at[tuple(index_at)].set(smallest).at[tuple(neighbour)].set(largest)


def raised(result, key, source, target, shards_of, factor):
    owner, partner = [(jnp.arange(result.shape[dim]) // (result.shape[dim] // shards_of)).reshape([-1 if axis == dim else 1 for axis in range(result.ndim)]) for dim in (source, target)]
    chosen = jax.random.permutation(key, shards_of)[partner]
    strong = (owner == chosen) | (owner == (partner + shards_of // 2) % shards_of)
    return jnp.where(strong, factor * result, result)


def level_of(stream_key, shape, pieces, low, high):
    def one(position, shards_of):
        heights = jax.random.uniform(jax.random.fold_in(jax.random.fold_in(stream_key, 6), position), (shards_of,), jnp.float32, low / len(pieces), high / len(pieces))
        return jnp.repeat(jnp.exp(heights), shape[position] // shards_of).reshape((-1,) + (1,) * (len(shape) - position - 1))

    loudness = one(*pieces[0])
    for cut in pieces[1:]:
        loudness = loudness * one(*cut)
    return loudness


def normal_values(stream_key, dims, scale, limit, split=(), kind=jnp.bfloat16):
    entries = scale * jax.random.normal(stream_key, dims, jnp.float32)
    if split:
        entries = entries * level_of(stream_key, dims, split, -0.22, 0.18)
    return jnp.clip(entries, -limit, limit).astype(kind)


def gaussian_with(own_key, shape, scale, reach, pieces, heavy, held_as=jnp.bfloat16):
    result = scale * jax.random.normal(own_key, shape, jnp.float32)
    if pieces:
        result = result * level_of(own_key, shape, pieces, -0.22, 0.18)
    return jnp.clip(raised(result, jax.random.fold_in(own_key, 3), *heavy), -reach, reach).astype(held_as)


def setup_inputs(seed: int = 0) -> dict:
    streams_of = jax.random.split(jax.random.key(seed), 7)
    control = normal_values(streams_of[0], (MEMBERS, LEV, NLAT, NLON), 1.0, 6.0, ((0, 4), (2, 2), (3, 4)))
    ens_pert = gaussian_with(streams_of[1], (MEMBERS, LEV, NLAT, NLON), 1.0, 6.0, ((0, 4), (2, 2), (3, 4)), (0, 1, 4, 2.0))
    vertical_mix = normal_values(streams_of[2], (LEV, LEV), LEV ** -0.5, 0.875)
    obs_values = normal_values(streams_of[3], (TILES, TILES, LEV, CAP), 1.0, 6.0, ((0, 8),))
    obs_cells = set_ends(jax.random.randint(streams_of[4], (TILES, TILES, CAP), 0, CELLS), jax.random.fold_in(streams_of[4], 1), 0, CELLS - 1).astype(jnp.int32)
    obs_counts = draw_obs_counts(jax.random.fold_in(streams_of[6], 71), 0)
    return dict(control=control, ens_pert=ens_pert, vertical_mix=vertical_mix, obs_values=obs_values, obs_cells=obs_cells, obs_counts=obs_counts)


def taper_weights(distance):
    spread = HALF / 3.0
    total = sum((math.exp(-(offset / spread) ** 2) for offset in range(-HALF, HALF + 1)))
    values = jnp.exp(-0.5 * (distance / spread) ** 2) / math.sqrt(total)
    return jnp.where(jnp.abs(distance) <= HALF, values, 0.0).astype(jnp.bfloat16)

def reference(control, ens_pert, vertical_mix, obs_values, obs_cells, obs_counts):
    slot_ids = jnp.arange(CAP, dtype=jnp.int32)

    def per_tile(tile):
        values = obs_values[:, tile].astype(jnp.float32)
        cells = obs_cells[:, tile]
        live_mask = slot_ids[None, :] < obs_counts[:, tile][:, None]
        masked = jnp.where(live_mask[:, None, :], values, jnp.float32(0.0))
        flattened = jnp.transpose(masked, (1, 0, 2)).reshape(LEV, TILES * CAP)
        return jnp.zeros((LEV, CELLS), jnp.float32).at[:, cells.reshape(-1)].add(flattened)
    tiled = lax.map(per_tile, jnp.arange(TILES, dtype=jnp.int32))
    tiled = tiled.reshape(N_LAT, N_LON, LEV, LATD, LOND)
    adjoint = jnp.transpose(tiled, (2, 0, 3, 1, 4)).reshape(LEV, NLAT, NLON)
    pert32 = ens_pert.astype(jnp.float32)
    forcing = (pert32 * adjoint[None]).astype(jnp.bfloat16)
    mix32 = vertical_mix.astype(jnp.float32)
    vert_control = jnp.einsum('lm,kmac->klac', mix32, control.astype(jnp.float32)).astype(jnp.bfloat16)
    vert_forcing = jnp.einsum('ml,kmac->klac', mix32, forcing.astype(jnp.float32)).astype(jnp.bfloat16)
    fields = jnp.concatenate([vert_control, vert_forcing], axis=0)
    row_ids = jnp.arange(NLAT, dtype=jnp.int32)
    lat_kernel = taper_weights((row_ids[:, None] - row_ids[None, :]).astype(jnp.float32))
    lat_smooth = jnp.einsum('rn,flnc->flrc', lat_kernel.astype(jnp.float32), fields.astype(jnp.float32)).astype(jnp.bfloat16)
    col_ids = jnp.arange(NLON, dtype=jnp.int32)
    delta = (col_ids[:, None] - col_ids[None, :] + NLON // 2) % NLON - NLON // 2
    lon_kernel = taper_weights(delta.astype(jnp.float32))
    smooth = jnp.einsum('flap,pi->flai', lat_smooth.astype(jnp.float32), lon_kernel.astype(jnp.float32))
    increment = lax.optimization_barrier(jnp.sum(pert32 * smooth[:MEMBERS], axis=0))
    gradient = control.astype(jnp.float32) + smooth[MEMBERS:]
    return (increment, gradient)
```

```python
import functools
import math

import jax
import jax.numpy as jnp
import numpy as np
from jax import lax
from jax.experimental import pallas as pl
from jax.experimental.pallas import tpu as pltpu
from jax.sharding import PartitionSpec as P

HALF = 24
LANES = 128
CHUNKS = 3
MESH = pl.DeviceIdType.MESH
F32 = jnp.float32
BF16 = jnp.bfloat16


def taper_table(distance):
    spread = HALF / 3.0
    total = sum((math.exp(-((offset / spread) ** 2)) for offset in range(-HALF, HALF + 1)))
    values = np.exp(-0.5 * (distance / spread) ** 2) / math.sqrt(total)
    return np.where(np.abs(distance) <= HALF, values, 0.0).astype(np.float32)


def group_of(levels, rows):
    return max(g for g in range(1, levels + 1) if levels % g == 0 and g * rows <= 256)


def constants(levels, rows, cols):
    size = levels * rows
    index = np.arange(size)
    level_of = (index[:, None] // rows == np.arange(levels)[None, :]).astype(np.float32)
    row_of = (index[:, None] % rows == np.arange(rows)[None, :]).astype(np.float32)
    group = group_of(levels, rows)
    eye = np.eye(group, dtype=np.float32)
    r = np.arange(rows)
    delta = (r[:, None] - r[None, :]).astype(np.float64)
    lat_w = np.stack([np.kron(eye, taper_table(delta + s * rows)) for s in (0, 1, -1)])
    c = np.arange(cols)
    band = taper_table((c[:, None] - c[None, :]).astype(np.float64))
    slots = LANES // 32
    pack = np.zeros((2, slots * LANES, LANES), np.float32)
    halo_w = np.zeros((2, LANES, slots * LANES), np.float32)
    i = np.arange(LANES).astype(np.float64)
    for g in range(slots):
        for k in range(HALF):
            pack[0, g * LANES + k, 32 * g + k] = 1.0
            pack[1, g * LANES + LANES - HALF + k, 32 * g + k] = 1.0
            at = slice(g * LANES, (g + 1) * LANES)
            halo_w[0, 32 * g + k, at] = taper_table(k - HALF - i)
            halo_w[1, 32 * g + k, at] = taper_table(LANES + k - i)
    return [jnp.asarray(a, BF16) for a in (level_of, row_of, lat_w, band, pack, halo_w)]


def kernel(
    dims,
    control_h, pert_h, mix, values, cells, counts, level_h, row_h, lat_h, band_h, pack_h, halo_h,
    increment_h, gradient_h,
    control, pert, level_of, row_of, lat_w, band, pack, halo_w,
    live, got_v, got_c, loc_v, loc_c, kron_c, kron_f, lhs, rhs, val32, adjoint, field, field_l,
    field_v, halo,
    smoothed, edge_out, edge_in, inc32, part_out, part_in, total_out, grad,
    in_s, s1, s2, r2, loc_s, loc_r, lat_s, lat_r, lon_s, lon_r, rs_s, rs_r, out_s,
):
    levels, rows, cols, members, n_lat, n_lon, tiles, cap = dims
    size = levels * rows
    parts = members // n_lat
    half = cap // parts
    away = n_lon - 1
    mem, lat, lon = lax.axis_index("mem"), lax.axis_index("lat"), lax.axis_index("lon")
    tile = lat * n_lon + lon
    slots = LANES // 32
    group = group_of(levels, rows)
    block = group * rows
    chunk = size // CHUNKS
    packed = chunk // slots

    def dot(a, b, dims=(((1,), (0,)), ((), ()))):
        return lax.dot_general(a, b, dims, preferred_element_type=F32)

    nt = (((1,), (1,)), ((), ()))

    inputs = [
        pltpu.make_async_copy(src, dst, in_s.at[i])
        for i, (src, dst) in enumerate((
            (level_h, level_of), (row_h, row_of), (control_h, control), (lat_h, lat_w),
            (pack_h, pack), (band_h, band), (halo_h, halo_w), (pert_h, pert),
        ))
    ]
    for copy in inputs:
        copy.start()

    slot = lax.broadcasted_iota(jnp.int32, (1, half), 1)
    for t in range(tiles):
        for h in range(parts):
            live[t, h] = jnp.where(
                slot + h * half < counts[0, t], cells[t : t + 1, h * half : (h + 1) * half], -1
            )

    barrier = pltpu.get_barrier_semaphore()
    for d in range(1, tiles):
        other = lax.rem(tile + d, tiles)
        pl.semaphore_signal(
            barrier, inc=1, device_id_type=MESH,
            device_id={"lat": other // n_lon, "lon": lax.rem(other, n_lon)},
        )
    for d in range(1, members):
        pl.semaphore_signal(
            barrier, inc=1, device_id={"mem": lax.rem(mem + d, members)}, device_id_type=MESH
        )
    pl.semaphore_wait(barrier, tiles + members - 2)

    piece = lax.rem(mem, parts)
    other_lat = lax.rem(mem // parts - lat + 2 * n_lat, n_lat)

    def values_of(t, h):
        return values.at[t, :, pl.ds(pl.multiple_of(h * half, half), half)]

    def leg_one(o):
        other_lon = lax.rem(lon + o, n_lon)
        t = other_lat * n_lon + other_lon
        return [
            pltpu.make_async_remote_copy(
                src_ref=src, dst_ref=dst.at[mem, o - 1], send_sem=s1.at[o - 1, k],
                recv_sem=r2.at[mem, o - 1, k],
                device_id={"lat": other_lat, "lon": other_lon}, device_id_type=MESH,
            )
            for k, (src, dst) in enumerate(((values_of(t, piece), got_v), (live.at[t, piece], got_c)))
        ]

    def straight(d):
        target = lax.rem(lat + d, n_lat)
        t = target * n_lon + lon
        return [
            pltpu.make_async_remote_copy(
                src_ref=src, dst_ref=dst.at[d, h], send_sem=loc_s.at[d, h, k],
                recv_sem=loc_r.at[d, h, k], device_id={"lat": target}, device_id_type=MESH,
            )
            for h in range(parts)
            for k, (src, dst) in enumerate(((values_of(t, h), loc_v), (live.at[t, h], loc_c)))
        ]

    kept = [
        pltpu.make_async_copy(values_of(tile, h), loc_v.at[0, h], loc_r.at[0, h, 0])
        for h in range(parts)
    ]
    for o in sorted(range(1, n_lon), key=lambda o: -min(o, n_lon - o)):
        for copy in leg_one(o):
            copy.start()
    for d in range(1, n_lat):
        for copy in straight(d):
            copy.start()
    for copy in kept:
        copy.start()
    for h in range(parts):
        loc_c[0, h] = live[tile, h]

    def leg_two(d, p):
        return [
            pltpu.make_async_remote_copy(
                src_ref=buf.at[mem, p], dst_ref=buf.at[mem, p], send_sem=s2.at[d, p, k],
                recv_sem=r2.at[mem, p, k],
                device_id={"mem": lax.rem(mem + d, members)}, device_id_type=MESH,
            )
            for k, buf in enumerate((got_v, got_c))
        ]

    def arrived(owner, p):
        for k, buf in enumerate((got_v, got_c)):
            pltpu.make_async_remote_copy(
                src_ref=buf.at[owner, p], dst_ref=buf.at[owner, p], send_sem=s2.at[0, p, k],
                recv_sem=r2.at[owner, p, k],
                device_id={"mem": lax.rem(mem + 1, members)}, device_id_type=MESH,
            ).wait_recv()

    def build_kron(out, spread):
        step = size // 6

        def body(i, carry):
            at = pl.ds(pl.multiple_of(i * step, step), step)
            line = spread(level_of[at, :]).astype(BF16)
            full = dot(line, level_of[...], nt)
            same = dot(row_of[at, :], row_of[...], nt)
            out[at, :] = (full * same).astype(BF16)
            return carry

        lax.fori_loop(0, 6, body, 0)

    def vertical(kron, src, out, c):
        at = pl.ds(c * chunk, chunk)
        out[at, :] = dot(kron[at, :], src[...]).astype(BF16)

    if n_lat == 2:
        sides = [(None, None)]
    else:
        sides = [(1, 1), (-1, 2)]

    def lat_copy(f, q, c):
        shift = sides[q][0]
        target = 1 - lat if shift is None else lat + shift
        if f == 0:
            src, dst = control_h, halo.at[0, q]
        else:
            at = pl.ds(c * chunk, chunk)
            src, dst = field_v.at[at, :], halo.at[1, q, at, :]
        return pltpu.make_async_remote_copy(
            src_ref=src, dst_ref=dst, send_sem=lat_s.at[f, q, c], recv_sem=lat_r.at[f, q, c],
            device_id={"lat": target}, device_id_type=MESH,
        )

    def sends(q):
        shift = sides[q][0]
        return None if shift is None else (lat < n_lat - 1 if shift == 1 else lat > 0)

    def receives(q):
        shift = sides[q][0]
        return None if shift is None else (lat > 0 if shift == 1 else lat < n_lat - 1)

    def under(condition, run):
        if condition is None:
            run()
        else:
            pl.when(condition)(run)

    def lat_send(f, c):
        for q in range(len(sides)):
            under(sends(q), lat_copy(f, q, c).start)

    def lat_clear(f):
        for q in range(len(sides)):
            if sides[q][0] is not None:
                @pl.when(jnp.logical_not(receives(q)))
                def _():
                    halo[f, q] = jnp.zeros((size, cols), BF16)

    def lat_weights():
        weights = []
        for q in range(len(sides)):
            if sides[q][0] is None:
                weights.append(jnp.where(lat == 1, lat_w[1], lat_w[2]))
            else:
                weights.append(lat_w[sides[q][1]])
        return weights

    def lat_arrived(f, c):
        for q in range(len(sides)):
            under(receives(q), lat_copy(f, q, c).wait_recv)

    def lat_sum(f, src, out, weights, c):
        for g in range(c * chunk // block, (c + 1) * chunk // block):
            at = pl.ds(g * block, block)
            total = dot(lat_w[0], src[at, :])
            for q in range(len(sides)):
                total += dot(weights[q], halo[f, q, at, :])
            out[at, :] = total.astype(BF16)

    def lon_copy(f, q, c):
        target = lax.rem(lon + (n_lon - 1 if q == 0 else 1), n_lon)
        return pltpu.make_async_remote_copy(
            src_ref=edge_out.at[f, q, c], dst_ref=edge_in.at[f, q, c],
            send_sem=lon_s.at[f, q, c], recv_sem=lon_r.at[f, q, c],
            device_id={"lon": target}, device_id_type=MESH,
        )

    def lon_send(f, c):
        for q in range(2):
            low = 0 if q == 0 else cols - LANES
            wide = jnp.concatenate(
                [
                    smoothed[f, c * chunk + g * packed : c * chunk + (g + 1) * packed, low : low + LANES]
                    for g in range(slots)
                ],
                axis=1,
            )
            edge_out[f, q, c] = dot(wide, pack[q]).astype(BF16)
            lon_copy(f, q, c).start()

    def lon_sides(f, c):
        for q in range(2):
            lon_copy(f, q, c).wait_recv()

        def rows_of(edge, weight):
            flat = dot(edge, weight)
            return jnp.concatenate(
                [flat[:, g * LANES : (g + 1) * LANES] for g in range(slots)], axis=0
            )

        return rows_of(edge_in[f, 1, c], halo_w[0]), rows_of(edge_in[f, 0, c], halo_w[1])

    lat_send(0, 0)
    lat_clear(0)
    lat_clear(1)
    inputs[0].wait()
    inputs[1].wait()
    build_kron(kron_c, lambda e: dot(e, mix[...]))
    for copy in inputs[2:]:
        copy.wait()
    weights = lat_weights()
    lat_arrived(0, 0)
    for c in range(CHUNKS):
        lat_sum(0, control, field_l, weights, c)
    for c in range(CHUNKS):
        vertical(kron_c, field_l, smoothed.at[0], c)
        lon_send(0, c)

    for p in range(away):
        arrived(mem, p)
        for d in range(1, members):
            for copy in leg_two(d, p):
                copy.start()

    build_kron(kron_f, lambda e: dot(e, mix[...], nt))

    adjoint[...] = jnp.zeros((size, cols), F32)

    def scatter(blocks):
        for n, (val, cel) in enumerate(blocks):
            lanes = slice(n * half, (n + 1) * half)
            cell = cel.astype(F32)
            row = jnp.floor((cell + 0.5) * (1.0 / cols))
            col = cell - row * cols
            val32[...] = val.astype(F32)
            hit = lax.broadcasted_iota(jnp.int32, (rows, half), 0).astype(F32) == row

            def left(i, carry):
                two = [jnp.where(hit, val32[pl.ds(2 * i + k, 1), :], 0.0) for k in range(2)]
                at = pl.ds(pl.multiple_of(i * 2 * rows, 2 * rows), 2 * rows)
                lhs[at, lanes] = jnp.concatenate(two, axis=0).astype(BF16)
                return carry

            lax.fori_loop(0, levels // 2, left, 0)
            step = 64

            def right(i, carry):
                ids = (lax.broadcasted_iota(jnp.int32, (step, half), 0) + i * step).astype(F32)
                at = pl.ds(pl.multiple_of(i * step, step), step)
                rhs[at, lanes] = jnp.where(ids == col, 1.0, 0.0).astype(BF16)
                return carry

            lax.fori_loop(0, cols // step, right, 0)
        wide = len(blocks) * half

        def body(i, carry):
            at = pl.ds(pl.multiple_of(i * chunk, chunk), chunk)
            adjoint[at, :] += dot(lhs[at, :wide], rhs[:, :wide], nt)
            return carry

        lax.fori_loop(0, 3, body, 0)

    def near(d, carry):
        scatter([(loc_v[d, h], loc_c[d, h]) for h in range(parts)])
        return carry

    def far(owner):
        scatter([(got_v[owner, p], got_c[owner, p]) for p in range(away)])

    for copy in kept:
        copy.wait()
    for d in range(1, n_lat):
        for copy in straight(d):
            copy.wait_recv()
    lax.fori_loop(0, n_lat, near, 0)

    for c in range(CHUNKS):
        at = pl.ds(c * chunk, chunk)
        mid = dot(smoothed[0, at, :], band[...])
        left, right = lon_sides(0, c)
        smooth = jnp.concatenate(
            [mid[:, :LANES] + left, mid[:, LANES:-LANES], mid[:, -LANES:] + right], axis=1
        )
        inc32[at, :] = pert[at, :].astype(F32) * smooth
    part = size // members

    def rs_copy(d):
        target = lax.rem(mem + d, members)
        return pltpu.make_async_remote_copy(
            src_ref=part_out.at[d], dst_ref=part_in.at[d], send_sem=rs_s.at[d],
            recv_sem=rs_r.at[d], device_id={"mem": target}, device_id_type=MESH,
        )

    for d in range(1, members):
        at = pl.ds(pl.multiple_of(lax.rem(mem + d, members) * part, part), part)
        part_out[d] = inc32[at, :].astype(BF16)
        rs_copy(d).start()

    far(mem)

    def others(d, carry):
        owner = lax.rem(mem + members - d, members)
        for p in range(away):
            arrived(owner, p)
        far(owner)
        return carry

    lax.fori_loop(1, members - 1, others, 0)
    last = lax.rem(mem + 1, members)
    for p in range(away):
        arrived(last, p)
    far(last)

    field[...] = (pert[...].astype(F32) * adjoint[...]).astype(BF16)
    for c in range(CHUNKS):
        vertical(kron_f, field, field_v, c)
        lat_send(1, c)
    for c in range(CHUNKS):
        lat_arrived(1, c)
        lat_sum(1, field_v, smoothed.at[1], weights, c)
        lon_send(1, c)
    for c in range(CHUNKS):
        at = pl.ds(c * chunk, chunk)
        grad[at, :] = control[at, :].astype(F32) + dot(smoothed[1, at, :], band[...])

    total = inc32[pl.ds(pl.multiple_of(mem * part, part), part), :]
    for d in range(1, members):
        rs_copy(d).wait_recv()
        total += part_in[d].astype(F32)
    total_out[...] = total
    outputs = [pltpu.make_async_copy(total_out, increment_h, out_s.at[CHUNKS])]
    outputs[0].start()
    for c in range(CHUNKS):
        at = pl.ds(c * chunk, chunk)
        left, right = lon_sides(1, c)
        grad[at, :LANES] += left
        grad[at, cols - LANES :] += right
        outputs.append(pltpu.make_async_copy(grad.at[at, :], gradient_h.at[at, :], out_s.at[c]))
        outputs[-1].start()
    for copy in outputs:
        copy.wait()

    for o in range(1, n_lon):
        for copy in leg_one(o):
            copy.wait_send()
    for d in range(1, n_lat):
        for copy in straight(d):
            copy.wait_send()
    for p in range(away):
        for d in range(1, members):
            for copy in leg_two(d, p):
                copy.wait_send()
    for q in range(len(sides)):
        under(sends(q), lat_copy(0, q, 0).wait_send)
        for c in range(CHUNKS):
            under(sends(q), lat_copy(1, q, c).wait_send)
    for f in range(2):
        for q in range(2):
            for c in range(CHUNKS):
                lon_copy(f, q, c).wait_send()
    for d in range(1, members):
        rs_copy(d).wait_send()


def shards(sizes, control, ens_pert, vertical_mix, obs_values, obs_cells, obs_counts):
    members, n_lat, n_lon = sizes
    _, levels, rows, cols = control.shape
    tiles, cap = obs_values.shape[1], obs_values.shape[3]
    size = levels * rows
    parts = members // n_lat
    half = cap // parts
    away = n_lon - 1
    slots = LANES // 32
    packed = size // CHUNKS // slots
    sides = 1 if n_lat == 2 else 2
    part = size // members
    dims = (levels, rows, cols, members, n_lat, n_lon, tiles, cap)
    dma = pltpu.SemaphoreType.DMA
    vmem = pl.BlockSpec(memory_space=pltpu.VMEM)
    hbm = pl.BlockSpec(memory_space=pl.ANY)
    group = group_of(levels, rows) * rows
    wide = max(parts, away) * half
    scratch = [
        pltpu.VMEM((size, cols), BF16),
        pltpu.VMEM((size, cols), BF16),
        pltpu.VMEM((size, levels), BF16),
        pltpu.VMEM((size, rows), BF16),
        pltpu.VMEM((3, group, group), BF16),
        pltpu.VMEM((cols, cols), BF16),
        pltpu.VMEM((2, slots * LANES, LANES), BF16),
        pltpu.VMEM((2, LANES, slots * LANES), BF16),
        pltpu.VMEM((tiles, parts, 1, half), jnp.int32),
        pltpu.VMEM((members, away, levels, half), BF16),
        pltpu.VMEM((members, away, 1, half), jnp.int32),
        pltpu.VMEM((n_lat, parts, levels, half), BF16),
        pltpu.VMEM((n_lat, parts, 1, half), jnp.int32),
        pltpu.VMEM((size, size), BF16),
        pltpu.VMEM((size, size), BF16),
        pltpu.VMEM((size, wide), BF16),
        pltpu.VMEM((cols, wide), BF16),
        pltpu.VMEM((levels, half), F32),
        pltpu.VMEM((size, cols), F32),
        pltpu.VMEM((size, cols), BF16),
        pltpu.VMEM((size, cols), BF16),
        pltpu.VMEM((size, cols), BF16),
        pltpu.VMEM((2, sides, size, cols), BF16),
        pltpu.VMEM((2, size, cols), BF16),
        pltpu.VMEM((2, 2, CHUNKS, packed, LANES), BF16),
        pltpu.VMEM((2, 2, CHUNKS, packed, LANES), BF16),
        pltpu.VMEM((size, cols), F32),
        pltpu.VMEM((members, part, cols), BF16),
        pltpu.VMEM((members, part, cols), BF16),
        pltpu.VMEM((part, cols), F32),
        pltpu.VMEM((size, cols), F32),
        dma((8,)), dma((away, 2)), dma((members, away, 2)), dma((members, away, 2)),
        dma((n_lat, parts, 2)), dma((n_lat, parts, 2)),
        dma((2, sides, CHUNKS)), dma((2, sides, CHUNKS)), dma((2, 2, CHUNKS)), dma((2, 2, CHUNKS)),
        dma((members,)), dma((members,)), dma((CHUNKS + 1,)),
    ]
    control = control.reshape(size, cols)
    level_of, row_of, lat_w, band, pack, halo_w = constants(levels, rows, cols)
    increment, gradient = pl.pallas_call(
        functools.partial(kernel, dims),
        out_shape=(
            jax.ShapeDtypeStruct((part, cols), F32),
            jax.ShapeDtypeStruct((size, cols), F32),
        ),
        in_specs=[
            hbm, hbm, vmem, hbm, vmem, pl.BlockSpec(memory_space=pltpu.SMEM),
            hbm, hbm, hbm, hbm, hbm, hbm,
        ],
        out_specs=(hbm, hbm),
        scratch_shapes=scratch,
        compiler_params=pltpu.CompilerParams(
            collective_id=0, has_side_effects=True, vmem_limit_bytes=60 * 2**20
        ),
    )(
        control, ens_pert.reshape(size, cols), vertical_mix,
        obs_values.reshape(tiles, levels, cap), obs_cells.reshape(tiles, cap), obs_counts,
        level_of, row_of, lat_w, band, pack, halo_w,
    )
    return (
        increment.reshape(levels // members, rows, cols),
        gradient.reshape(1, levels, rows, cols),
    )


def solution(mesh):
    sizes = tuple(mesh.shape[a] for a in ("mem", "lat", "lon"))
    return jax.shard_map(
        functools.partial(shards, sizes),
        mesh=mesh,
        in_specs=(
            P("mem", None, "lat", "lon"),
            P("mem", None, "lat", "lon"),
            P(),
            P(("lat", "lon"), None, None, None),
            P(("lat", "lon"), None, None),
            P(("lat", "lon"), None),
        ),
        out_specs=(P("mem", "lat", "lon"), P("mem", None, "lat", "lon")),
        check_vma=False,
    )
```
